32 devices in a mesh: rep: 4 (over y, x), ctx: 8 (over z, core).
Axes of the slice: x: 2, y: 2, z: 4, core: 2. Of those that a mesh axis runs over, the one named last changes fastest.
Arguments:
- tokens: bfloat16 [4, 1024, 1024], P('rep', 'ctx'), may hold values from -6 to 6
- segment_ids: int32 [4, 1024], P('rep'), may hold values from 0 to 3, as said below
- positions: int32 [4, 1024], P('rep'), may hold values from 0 to 767, as said below
- cotangent: bfloat16 [4, 1024, 1024], P('rep', 'ctx'), may hold values from -6 to 6
- qkv_weight: bfloat16 [2, 1024, 4096], P(None, 'ctx'), may hold values from -0.1875 to 0.1875
- out_weight: bfloat16 [2, 2048, 1024], P(None, 'ctx'), may hold values from -0.5 to 0.5
- attn_gain: bfloat16 [2, 1024], P(None, 'ctx'), may hold values from 0.3984375 to 1.59375
- query_gain: bfloat16 [2, 128], P(None, 'ctx'), may hold values from 0.25 to 1.75
- key_gain: bfloat16 [2, 128], P(None, 'ctx'), may hold values from 0.25 to 1.75
- mlp_gain: bfloat16 [2, 1024], P(None, 'ctx'), may hold values from 0.3984375 to 1.59375
- gate_up_weight: bfloat16 [2, 1024, 6144], P(None, 'ctx'), may hold values from -0.1875 to 0.1875
- down_weight: bfloat16 [2, 3072, 1024], P(None, 'ctx'), may hold values from -0.21875 to 0.21875
Outputs:
- outputs: bfloat16 [4, 1024, 1024], P('rep', 'ctx')
- input_grad: float32 [4, 1024, 1024], P('rep', 'ctx')
- qkv_grad: float32 [2, 1024, 4096], P(None, 'ctx')
- out_grad: float32 [2, 2048, 1024], P(None, 'ctx')
- attn_gain_grad: float32 [2, 1024], P(None, 'ctx')
- query_gain_grad: float32 [2, 128], P(None, 'ctx')
- key_gain_grad: float32 [2, 128], P(None, 'ctx')
- mlp_gain_grad: float32 [2, 1024], P(None, 'ctx')
- gate_up_grad: float32 [2, 1024, 6144], P(None, 'ctx')
- down_grad: float32 [2, 3072, 1024], P(None, 'ctx')
The draws below stay inside these ranges and needn't reach their ends.
Inputs may be any that keep to these rules, and one draw needn't show every extreme that they name: `segment_ids`: each sequence packs four documents with ids 0, 1, 2, 3 in order, never falling; one document, the first or the last, has exactly 768 tokens. `positions`: the index of a token within its document: 0 at a document's first token, rising by one along it.
All inputs are finite; a program needn't handle non-finite values.
Results may differ from the reference program's by a relative error of at most 0.025.
Values may be sent and summed in bfloat16 or wider, within the bound.
No kernel may reach another device: no remote copies, remote signals or barrier semaphores. Data moves between devices by JAX's collectives and lax.ppermute only.
A program may use at most 384 MiB of HBM per device.

```python
import jax
import jax.numpy as jnp
from jax import lax

D = 1024
QUERY_HEADS = 16
KEY_VALUE_HEADS = 8
HEAD_SIZE = 128
FF = 3072
LAYERS = 2
SEQLEN = 1024
SEQS = 4
QKV = 4096


def doc_layout(key):
    folded = jax.random.fold_in(key, 11)
    longest = SEQLEN * 3 // 4
    quarter = SEQLEN - longest
    lowest = min(200, quarter // 6)
    highest = quarter // 2 - lowest // 2
    first_size = jax.random.randint(jax.random.fold_in(folded, 1), (SEQS, 1), lowest, highest)
    second_size = jax.random.randint(jax.random.fold_in(folded, 2), (SEQS, 1), lowest, highest)
    flipped = jax.random.randint(jax.random.fold_in(folded, 3), (SEQS, 1), 0, 2)
    start_one = jnp.where(flipped == 1, first_size, longest)
    start_two = jnp.where(flipped == 1, first_size + second_size, longest + first_size)
    start_three = jnp.where(flipped == 1, quarter, longest + first_size + second_size)
    offsets = jnp.arange(SEQLEN, dtype=jnp.int32)[None, :]
    past_first = (offsets >= start_one).astype(jnp.int32)
    past_second = (offsets >= start_two).astype(jnp.int32)
    past_third = (offsets >= start_three).astype(jnp.int32)
    segment = past_first + past_second + past_third
    doc_start = jnp.where(past_third == 1, start_three, jnp.where(past_second == 1, start_two, jnp.where(past_first == 1, start_one, 0)))
    return (segment.astype(jnp.int32), (offsets - doc_start).astype(jnp.int32))


def draw_segment_ids(key, part):
    return doc_layout(key)[0]


def draw_positions(key, part):
    return doc_layout(key)[1]


def levels(rng, dims, pieces, least, top_value):
    level = 1.0
    for axis_at, shards_of in pieces:
        heights = jax.random.uniform(jax.random.fold_in(jax.random.fold_in(rng, 6), axis_at), (shards_of,), jnp.float32, least / len(pieces), top_value / len(pieces))
        level = level * jnp.repeat(jnp.exp(heights), dims[axis_at] // shards_of).reshape((-1,) + (1,) * (len(dims) - 1 - axis_at))
    return level


def noise(rng, extent, spread, limit, pieces=(), held_as=jnp.bfloat16):
    loudness = levels(rng, extent, pieces, -0.22, 0.18) if pieces else 1.0
    values = jax.random.normal(rng, extent, jnp.float32) * spread * loudness
    return jnp.minimum(jnp.maximum(values, -limit), limit).astype(held_as)


def setup_inputs(seed: int = 0) -> dict:
    streams_of = jax.random.split(jax.random.key(seed), 13)
    tokens = noise(streams_of[0], (SEQS, SEQLEN, D), 1.0, 6.0, ((0, 4), (1, 8)))
    segment_ids = draw_segment_ids(jax.random.fold_in(streams_of[12], 71), 0)
    positions = draw_positions(jax.random.fold_in(streams_of[12], 71), 0)
    cotangent = noise(streams_of[3], (SEQS, SEQLEN, D), 1.0, 6.0, ((0, 4), (1, 8)))
    qkv_weight = noise(streams_of[4], (LAYERS, D, QKV), D ** -0.5, 0.1875, ((1, 8),))
    out_weight = noise(streams_of[5], (LAYERS, QUERY_HEADS * HEAD_SIZE, D), (QUERY_HEADS * HEAD_SIZE // 16) ** -0.5, 0.5, ((1, 8),))
    attn_gain = jnp.clip(1.0 + 0.12 * jax.random.normal(streams_of[6], (LAYERS, D), jnp.float32), 0.3984375, 1.59375).astype(jnp.bfloat16)
    query_gain = jnp.clip(1.0 + 0.15 * jax.random.normal(streams_of[7], (LAYERS, HEAD_SIZE), jnp.float32), 0.25, 1.75).astype(jnp.bfloat16)
    key_gain = jnp.clip(1.0 + 0.15 * jax.random.normal(streams_of[8], (LAYERS, HEAD_SIZE), jnp.float32), 0.25, 1.75).astype(jnp.bfloat16)
    mlp_gain = jnp.clip(1.0 + 0.12 * jax.random.normal(streams_of[9], (LAYERS, D), jnp.float32), 0.3984375, 1.59375).astype(jnp.bfloat16)
    gate_up_weight = noise(streams_of[10], (LAYERS, D, 2 * FF), D ** -0.5, 0.1875, ((1, 8),))
    down_weight = noise(streams_of[11], (LAYERS, FF, D), (FF // 4) ** -0.5, 0.21875, ((1, 8),))
    return dict(tokens=tokens, segment_ids=segment_ids, positions=positions, cotangent=cotangent, qkv_weight=qkv_weight, out_weight=out_weight, attn_gain=attn_gain, query_gain=query_gain, key_gain=key_gain, mlp_gain=mlp_gain, gate_up_weight=gate_up_weight, down_weight=down_weight)


EPS = 1e-06
THETA = 1000000.0

@jax.custom_vjp
def low(v):
    return lax.optimization_barrier(v.astype(jnp.bfloat16)).astype(jnp.float32)

@jax.custom_vjp
def low_back(v):
    return v

def low_keep(v):
    return (low(v), None)

def low_pass(kept, grad):
    return (grad,)

def back_keep(v):
    return (v, None)

def back_low(kept, grad):
    return (low(grad),)
low.defvjp(low_keep, low_pass)
low_back.defvjp(back_keep, back_low)

def root_mean_square_norm(inputs, scale_gain):
    return inputs * lax.rsqrt(lax.optimization_barrier(jnp.mean(inputs * inputs, axis=-1, keepdims=True)) + EPS) * scale_gain

def rotary_apply(inputs, cosine_table, sine_table):
    half_width = inputs.shape[-1] // 2
    turned = jnp.concatenate([-inputs[..., half_width:], inputs[..., :half_width]], axis=-1)
    return inputs * cosine_table + turned * sine_table

def phases(token_pos, width):
    frequency = THETA ** (-(jnp.arange(width // 2).astype(jnp.float32) * 2.0) / width)
    angle = token_pos.astype(jnp.float32)[:, None] * frequency[None, :]
    angle = jnp.concatenate([angle, angle], axis=-1)
    return (jnp.cos(angle)[:, None, :], jnp.sin(angle)[:, None, :])

def matmul_hi(left, right):
    return jnp.dot(left, right, preferred_element_type=jnp.float32, precision=lax.Precision.HIGHEST)

def one_layer(stream, segments, cosine_table, sine_table, w_qkv, w_out, gain_a, gain_q, key_gain_vector, gain_m, w_gu, w_down):
    sequence_length = stream.shape[0]
    normed = low(root_mean_square_norm(stream, gain_a))
    projected_rows = low_back(matmul_hi(normed, w_qkv))
    query_matrix = root_mean_square_norm(projected_rows[:, :QUERY_HEADS * HEAD_SIZE].reshape(sequence_length, QUERY_HEADS, HEAD_SIZE), gain_q)
    rows_of_keys = root_mean_square_norm(projected_rows[:, QUERY_HEADS * HEAD_SIZE:(QUERY_HEADS + KEY_VALUE_HEADS) * HEAD_SIZE].reshape(sequence_length, KEY_VALUE_HEADS, HEAD_SIZE), key_gain_vector)
    query_matrix = low(rotary_apply(query_matrix, cosine_table, sine_table)).reshape(sequence_length, KEY_VALUE_HEADS, QUERY_HEADS // KEY_VALUE_HEADS, HEAD_SIZE)
    rows_of_keys = low(rotary_apply(rows_of_keys, cosine_table, sine_table))
    rows_of_values = low(projected_rows[:, (QUERY_HEADS + KEY_VALUE_HEADS) * HEAD_SIZE:]).reshape(sequence_length, KEY_VALUE_HEADS, HEAD_SIZE)
    scores = jnp.einsum('tkgd,skd->kgts', query_matrix, rows_of_keys, precision=lax.Precision.HIGHEST)
    scores = low_back(scores * HEAD_SIZE ** (-0.5))
    places = jnp.arange(sequence_length, dtype=jnp.int32)
    allowed = (segments[:, None] == segments[None, :]) & (places[:, None] >= places[None, :])
    scores = jnp.where(allowed, scores, -1e+30)
    row_max = lax.optimization_barrier(jnp.max(scores, axis=-1, keepdims=True))
    expo_vals = jnp.exp(scores - row_max)
    probabilities = low(expo_vals / lax.optimization_barrier(jnp.sum(expo_vals, axis=-1, keepdims=True)))
    attended = jnp.einsum('kgts,skd->tkgd', probabilities, rows_of_values, precision=lax.Precision.HIGHEST)
    attended = low_back(low(attended.reshape(sequence_length, QUERY_HEADS * HEAD_SIZE)))
    middle = stream + low_back(matmul_hi(attended, w_out))
    normed_mid = low(root_mean_square_norm(middle, gain_m))
    gate_up = low_back(matmul_hi(normed_mid, w_gu))
    hidden = low(jax.nn.silu(gate_up[:, :FF]) * gate_up[:, FF:])
    return middle + low_back(matmul_hi(hidden, w_down))

def reference(tokens, segment_ids, positions, cotangent, qkv_weight, out_weight, attn_gain, query_gain, key_gain, mlp_gain, gate_up_weight, down_weight):
    weights_f32 = tuple((weight.astype(jnp.float32) for weight in (qkv_weight, out_weight, attn_gain, query_gain, key_gain, mlp_gain, gate_up_weight, down_weight)))
    layer_fn = jax.checkpoint(one_layer)

    def per_sequence(running, sequence):
        stream, segments, token_pos, seq_cotangent = sequence
        cosine_table, sine_table = phases(token_pos, HEAD_SIZE)

        def forward(initial, params):
            current = initial
            for which_layer in range(LAYERS):
                current = layer_fn(current, segments, cosine_table, sine_table, *[entry[which_layer] for entry in params])
            return current
        result, backward_function = jax.vjp(forward, stream.astype(jnp.float32), weights_f32)
        d_stream, d_weights = backward_function(seq_cotangent.astype(jnp.float32))
        running = jax.tree.map(lambda first_term, second_term: first_term + second_term, running, d_weights)
        return (running, (result.astype(jnp.bfloat16), d_stream))
    initial = jax.tree.map(jnp.zeros_like, weights_f32)
    totals, (outputs, input_grad) = lax.scan(per_sequence, initial, (tokens, segment_ids, positions, cotangent))
    return (outputs, input_grad, totals[0], totals[1], totals[2], totals[3], totals[4], totals[5], totals[6], totals[7])
```

```python
from functools import partial

import jax
import jax.numpy as jnp
from jax import lax
from jax.experimental import pallas as pl
from jax.experimental.pallas import tpu as pltpu
from jax.sharding import PartitionSpec as P

QUERY_HEADS = 16
KEY_VALUE_HEADS = 8
GROUP = QUERY_HEADS // KEY_VALUE_HEADS
HEAD = 128
EPS = 1e-06
THETA = 1000000.0
SCALE = HEAD**-0.5
BF = jnp.bfloat16
F32 = jnp.float32
AXES = ("rep", "ctx")
VMEM_LIMIT = 56 * 1024 * 1024


def dot(a, b):
    return jnp.dot(a, b, preferred_element_type=F32)


def dot_rows(a, b):
    return lax.dot_general(a, b, (((0,), (0,)), ((), ())), preferred_element_type=F32)


def dot_cols(a, b):
    return lax.dot_general(a, b, (((1,), (1,)), ((), ())), preferred_element_type=F32)


class Moves:
    def __init__(self, reps, ctxs):
        self.reps, self.ctxs = reps, ctxs
        at = lambda r, z, c: r * ctxs + 2 * z + c
        every = [(r, z, c) for r in range(reps) for z in range(ctxs // 2) for c in range(2)]
        self.swap = [(at(r, z, c), at(z, r, c)) for r, z, c in every]
        self.other = [(at(r, z, c), at(r, z, 1 - c)) for r, z, c in every]
        self.peer = [[(at(r, z, c), at(r ^ d, z, c)) for r, z, c in every] for d in range(reps)]
        self.order = sorted(range(1, reps), key=lambda d: -bin(d).count("1"))

    def turn(self, value):
        return lax.ppermute(value, AXES, self.swap)

    def sibling(self, value):
        return lax.ppermute(value, AXES, self.other)

    def gather(self, value):
        pieces = [value] + [None] * (self.reps - 1)
        for d in self.order:
            pieces[d] = lax.ppermute(value, AXES, self.peer[d])
        return pieces

    def scatter(self, make):
        got = [lax.ppermute(make(d).astype(BF), AXES, self.peer[d]) for d in self.order]
        total = make(0)
        for term in got:
            total = total + term.astype(F32)
        return total


def whole(*shape):
    return pl.BlockSpec(shape, lambda *_: (0,) * len(shape))


def rotate(v, cosine, sine):
    return v * cosine + pltpu.roll(v, HEAD // 2, 1) * sine


def rotate_back(d, cosine, sine):
    return d * cosine + pltpu.roll(d * sine, HEAD // 2, 1)


def qkv_body(pieces, nq, nk, *refs):
    xs, (w, qg, kg, cs, sn, q_out, kv_out, proj_out, held) = refs[:pieces], refs[pieces:]
    t = xs[0].shape[0]
    for j in range(pieces):
        held[j * t : (j + 1) * t, :] = xs[j][...]
    x = held[...]
    cosine, sine = cs[...], sn[...]
    heads = nq + 2 * nk
    for h in range(0, heads, 2):
        wide = min(2, heads - h)
        y2 = dot(x, w[:, h * HEAD : (h + wide) * HEAD])
        for i in range(wide):
            y = y2[:, i * HEAD : (i + 1) * HEAD]
            n = h + i
            if n < nq + nk:
                proj_out[:, n * HEAD : (n + 1) * HEAD] = y
                gain = (qg if n < nq else kg)[...]
                y = y * lax.rsqrt(jnp.mean(y * y, axis=-1, keepdims=True) + EPS) * gain
                y = rotate(y, cosine, sine)
            if n < nq:
                q_out[:, n * HEAD : (n + 1) * HEAD] = y.astype(BF)
            else:
                kv_out[:, (n - nq) * HEAD : (n - nq + 1) * HEAD] = y.astype(BF)


def qkv_call(xs, w, qg, kg, cs, sn, nq, nk):
    t, d = xs[0].shape
    n = t * len(xs)
    return pl.pallas_call(
        partial(qkv_body, len(xs), nq, nk),
        out_shape=(
            jax.ShapeDtypeStruct((n, nq * HEAD), BF),
            jax.ShapeDtypeStruct((n, 2 * nk * HEAD), BF),
            jax.ShapeDtypeStruct((n, (nq + nk) * HEAD), F32),
        ),
        scratch_shapes=[pltpu.VMEM((n, d), BF)],
        compiler_params=pltpu.CompilerParams(vmem_limit_bytes=VMEM_LIMIT),
        cost_estimate=pl.CostEstimate(
            flops=2 * n * d * (nq + 2 * nk) * HEAD, transcendentals=0, bytes_accessed=8 << 20
        ),
        name="qkv",
    )(*xs, w, qg, kg, cs, sn)


def fill(place, own, sib, dst, reps, t):
    r, c = place[0], place[1]
    for kk in range(reps):
        blk = pl.multiple_of((kk ^ r) * t, t)
        dst[pl.ds(pl.multiple_of((2 * kk + c) * t, t), t), :] = own[pl.ds(blk, t), :]
        dst[pl.ds(pl.multiple_of((2 * kk + 1 - c) * t, t), t), :] = sib[pl.ds(blk, t), :]


def stacked(ref, blk, t):
    rows = ref[pl.ds(blk, t), :]
    return jnp.concatenate([rows[:, i * HEAD : (i + 1) * HEAD] for i in range(GROUP)], axis=0)


def masked_scores(place, q, keys, segk, segq, kk, t):
    length = 2 * t * (kk + 1)
    s = dot_cols(q, keys[:length, :]) * SCALE
    mine = segq[kk * t : (kk + 1) * t, :]
    col = lax.broadcasted_iota(jnp.int32, (t, length), 1)
    row = lax.broadcasted_iota(jnp.int32, (t, length), 0) + (2 * kk + place[1]) * t
    same = jnp.concatenate([mine] * (length // HEAD), axis=1) == segk[:, :length]
    ok = same & (col <= row)
    ok = jnp.concatenate([ok.astype(F32)] * GROUP, axis=0) > 0.5
    return jnp.where(ok, s, -1e30)


def attend_body(reps, t, place, q, ko, vo, ks, vs, segk, segq, out, keys, values):
    fill(place, ko, ks, keys, reps, t)
    fill(place, vo, vs, values, reps, t)
    for kk in range(reps):
        blk = pl.multiple_of((kk ^ place[0]) * t, t)
        length = 2 * t * (kk + 1)
        s = masked_scores(place, stacked(q, blk, t), keys, segk, segq, kk, t)
        p = jnp.exp(s - jnp.max(s, axis=-1, keepdims=True))
        p = p * (1.0 / jnp.sum(p, axis=-1, keepdims=True))
        o = dot(p.astype(BF), values[:length, :])
        for i in range(GROUP):
            out[pl.ds(blk, t), i * HEAD : (i + 1) * HEAD] = o[i * t : (i + 1) * t, :].astype(BF)


def head_specs(n, nk):
    wide = pl.BlockSpec((n, GROUP * HEAD), lambda g, _: (0, g))
    key = pl.BlockSpec((n, HEAD), lambda g, _: (0, g))
    value = pl.BlockSpec((n, HEAD), lambda g, _: (0, nk + g))
    return wide, key, value


def attend_call(place, q, kv, kv_sib, segk, segq, reps, nk):
    n = q.shape[0]
    t = n // reps
    wide, key, value = head_specs(n, nk)
    return pl.pallas_call(
        partial(attend_body, reps, t),
        out_shape=jax.ShapeDtypeStruct(q.shape, BF),
        grid_spec=pltpu.PrefetchScalarGridSpec(
            num_scalar_prefetch=1,
            grid=(nk,),
            in_specs=[wide, key, value, key, value, whole(*segk.shape), whole(*segq.shape)],
            out_specs=wide,
            scratch_shapes=[pltpu.VMEM((2 * n, HEAD), BF)] * 2,
        ),
        compiler_params=pltpu.CompilerParams(vmem_limit_bytes=VMEM_LIMIT),
        cost_estimate=pl.CostEstimate(
            flops=4 * n * 2 * n * HEAD * nk * GROUP, transcendentals=2 * n * n * nk, bytes_accessed=4 << 20
        ),
        name="attend",
    )(place, q, kv, kv, kv_sib, kv_sib, segk, segq)


def attend_back_body(
    reps, t, place, q, ko, vo, ks, vs, do, segk, segq, dq, dko, dvo, dks, dvs, keys, values, dkeys, dvalues
):
    fill(place, ko, ks, keys, reps, t)
    fill(place, vo, vs, values, reps, t)
    for kk in reversed(range(reps)):
        blk = pl.multiple_of((kk ^ place[0]) * t, t)
        length = 2 * t * (kk + 1)
        qs = stacked(q, blk, t)
        dos = stacked(do, blk, t)
        s = masked_scores(place, qs, keys, segk, segq, kk, t)
        p = jnp.exp(s - jnp.max(s, axis=-1, keepdims=True))
        p = p * (1.0 / jnp.sum(p, axis=-1, keepdims=True))
        dp = dot_cols(dos, values[:length, :])
        delta = jnp.sum(p * dp, axis=-1, keepdims=True)
        ds = (p * (dp - delta)).astype(BF)
        o = dot(ds, keys[:length, :]) * SCALE
        for i in range(GROUP):
            dq[pl.ds(blk, t), i * HEAD : (i + 1) * HEAD] = o[i * t : (i + 1) * t, :]
        dk = dot_rows(ds, qs) * SCALE
        dv = dot_rows(p.astype(BF), dos)
        if kk == reps - 1:
            dkeys[...] = dk
            dvalues[...] = dv
        else:
            dkeys[:length, :] += dk
            dvalues[:length, :] += dv
    r, c = place[0], place[1]
    for kk in range(reps):
        blk = pl.multiple_of((kk ^ r) * t, t)
        mine = pl.ds(pl.multiple_of((2 * kk + c) * t, t), t)
        theirs = pl.ds(pl.multiple_of((2 * kk + 1 - c) * t, t), t)
        dko[pl.ds(blk, t), :] = dkeys[mine, :]
        dvo[pl.ds(blk, t), :] = dvalues[mine, :]
        dks[pl.ds(blk, t), :] = dkeys[theirs, :].astype(BF)
        dvs[pl.ds(blk, t), :] = dvalues[theirs, :].astype(BF)


def attend_back_call(place, q, kv, kv_sib, do, segk, segq, reps, nk):
    n = q.shape[0]
    t = n // reps
    wide, key, value = head_specs(n, nk)
    narrow = jax.ShapeDtypeStruct((n, nk * HEAD), F32)
    narrow_b = jax.ShapeDtypeStruct((n, nk * HEAD), BF)
    return pl.pallas_call(
        partial(attend_back_body, reps, t),
        out_shape=(jax.ShapeDtypeStruct(q.shape, F32), narrow, narrow, narrow_b, narrow_b),
        grid_spec=pltpu.PrefetchScalarGridSpec(
            num_scalar_prefetch=1,
            grid=(nk,),
            in_specs=[wide, key, value, key, value, wide, whole(*segk.shape), whole(*segq.shape)],
            out_specs=(wide, key, key, key, key),
            scratch_shapes=[pltpu.VMEM((2 * n, HEAD), BF)] * 2 + [pltpu.VMEM((2 * n, HEAD), F32)] * 2,
        ),
        compiler_params=pltpu.CompilerParams(vmem_limit_bytes=VMEM_LIMIT),
        cost_estimate=pl.CostEstimate(
            flops=10 * n * 2 * n * HEAD * nk * GROUP, transcendentals=2 * n * n * nk, bytes_accessed=8 << 20
        ),
        name="attend_back",
    )(place, q, kv, kv, kv_sib, kv_sib, do, segk, segq)


def head_back_body(nq, nk, dq, dko, dvo, dks, dvs, proj, cs, sn, qg, kg, out, dqg, dkg):
    @pl.when(pl.program_id(0) == 0)
    def _():
        dqg[...] = jnp.zeros_like(dqg)
        dkg[...] = jnp.zeros_like(dkg)

    cosine, sine = cs[...], sn[...]
    for n in range(nq + nk):
        at = slice(n * HEAD, (n + 1) * HEAD)
        if n < nq:
            d, gain, total = dq[:, at], qg[...], dqg
        else:
            part = slice((n - nq) * HEAD, (n - nq + 1) * HEAD)
            d, gain, total = dko[:, part] + dks[:, part].astype(F32), kg[...], dkg
        dy = rotate_back(d, cosine, sine)
        v = proj[:, at]
        rs = lax.rsqrt(jnp.mean(v * v, axis=-1, keepdims=True) + EPS)
        hat = v * rs
        gdy = dy * gain
        dv = rs * (gdy - hat * jnp.mean(hat * gdy, axis=-1, keepdims=True))
        out[:, at] = dv.astype(BF)
        total[...] += jnp.sum(dy * hat, axis=0, keepdims=True)
    first = (nq + nk) * HEAD
    out[:, first:] = (dvo[...] + dvs[...].astype(F32)).astype(BF)


def head_back_call(dq, dko, dvo, dks, dvs, proj, cs, sn, qg, kg, reps, nq, nk):
    n = dq.shape[0]
    t = n // reps
    rows = lambda width: pl.BlockSpec((t, width), lambda i: (i, 0))
    gain = jax.ShapeDtypeStruct((1, HEAD), F32)
    return pl.pallas_call(
        partial(head_back_body, nq, nk),
        out_shape=(jax.ShapeDtypeStruct((n, (nq + 2 * nk) * HEAD), BF), gain, gain),
        grid=(reps,),
        in_specs=[
            rows(nq * HEAD),
            *[rows(nk * HEAD)] * 4,
            rows((nq + nk) * HEAD),
            rows(HEAD),
            rows(HEAD),
            whole(1, HEAD),
            whole(1, HEAD),
        ],
        out_specs=(rows((nq + 2 * nk) * HEAD), whole(1, HEAD), whole(1, HEAD)),
        compiler_params=pltpu.CompilerParams(vmem_limit_bytes=VMEM_LIMIT),
        cost_estimate=pl.CostEstimate(flops=n * nq * HEAD * 40, transcendentals=0, bytes_accessed=8 << 20),
        name="head_back",
    )(dq, dko, dvo, dks, dvs, proj, cs, sn, qg, kg)


def rms(x):
    return lax.rsqrt(jnp.mean(x * x, axis=-1, keepdims=True) + EPS)


def rms_back(x, gain, dy):
    rs = rms(x)
    gdy = dy * gain
    return rs * gdy - x * (rs * rs * rs) * jnp.mean(x * gdy, axis=-1, keepdims=True)


def local(reps, ctxs, tokens, segment_ids, positions, cotangent, qkv_weight, out_weight, attn_gain, query_gain,
          key_gain, mlp_gain, gate_up_weight, down_weight):
    move = Moves(reps, ctxs)
    line = ctxs // 2
    layers, d_rows, qkv_cols = qkv_weight.shape
    width = tokens.shape[2]
    t = tokens.shape[1]
    n = reps * t
    ff = gate_up_weight.shape[2] // 2
    ffr = ff // reps
    nq, nk = QUERY_HEADS // reps, KEY_VALUE_HEADS // reps
    out_rows, down_rows = out_weight.shape[1] // reps, down_weight.shape[1] // reps
    r = lax.axis_index("rep")
    core = lax.axis_index("ctx") % 2
    place = jnp.stack([r, core]).astype(jnp.int32)

    x = move.turn(tokens[0])
    marks = move.turn(jnp.concatenate([segment_ids, positions], axis=0))
    top = move.turn(cotangent[0])
    gains = lax.all_gather(
        jnp.concatenate([attn_gain, mlp_gain, query_gain, key_gain], axis=1), "ctx", axis=0
    ).astype(F32)
    at = 0
    gain_sets = []
    for size in (d_rows, d_rows, HEAD // ctxs, HEAD // ctxs):
        part = gains[:, :, at : at + size]
        gain_sets.append(part.transpose(1, 0, 2).reshape(layers, 1, ctxs * size))
        at += size
    gain_a, gain_m, gain_q, gain_k = gain_sets

    def columns(l):
        sl = lambda w, start, size: lax.dynamic_slice(w, (0, start + r * size), (d_rows, size))
        w, gu = qkv_weight[l], gate_up_weight[l]
        qkv = jnp.concatenate(
            [
                sl(w, 0, nq * HEAD),
                sl(w, QUERY_HEADS * HEAD, nk * HEAD),
                sl(w, (QUERY_HEADS + KEY_VALUE_HEADS) * HEAD, nk * HEAD),
            ],
            axis=1,
        )
        gate_up = jnp.concatenate([sl(gu, 0, ffr), sl(gu, ff, ffr)], axis=1)
        return qkv, gate_up

    def rows(l):
        piece = jnp.concatenate(
            [
                lax.dynamic_slice(out_weight[l], (r * out_rows, 0), (out_rows, width)),
                lax.dynamic_slice(down_weight[l], (r * down_rows, 0), (down_rows, width)),
            ],
            axis=0,
        )
        return move.turn(piece)

    def by_core(piece):
        size = piece.shape[1]
        return piece.reshape(line, 2, size, width).transpose(1, 0, 2, 3).reshape(ctxs * size, width)

    def by_place(value):
        size = value.shape[0] // ctxs
        return value.reshape(2, line, size, width).transpose(1, 0, 2, 3).reshape(ctxs, size, width)

    weights = []
    row_pieces = [rows(l) for l in range(layers)]
    for l in range(layers):
        qkv, gate_up = columns(l)
        w_qkv = lax.all_gather(qkv, "ctx", axis=0, tiled=True)
        w_rows = lax.all_gather(row_pieces[l], "ctx", axis=0)
        w_gu = lax.all_gather(gate_up, "ctx", axis=0, tiled=True)
        weights.append((w_qkv, by_core(w_rows[:, :out_rows]), w_gu, by_core(w_rows[:, out_rows:])))

    seg_all, pos_all = marks[0], marks[1]
    slice_of = lambda v, k: lax.dynamic_slice(v, ((2 * k + core) * t,), (t,))
    pos_mine = jnp.concatenate([slice_of(pos_all, j ^ r) for j in range(reps)])
    seg_mine = jnp.concatenate([slice_of(seg_all, k) for k in range(reps)])
    segk = seg_all[None, :]
    segq = jnp.broadcast_to(seg_mine[:, None], (n, HEAD))
    frequency = THETA ** (-(jnp.arange(HEAD // 2).astype(F32) * 2.0) / HEAD)
    angle = pos_mine.astype(F32)[:, None] * frequency[None, :]
    cosine, sine = jnp.cos(angle), jnp.sin(angle)
    cs = jnp.concatenate([cosine, cosine], axis=1)
    sn = jnp.concatenate([-sine, sine], axis=1)

    x = x.astype(F32)
    saved = []
    for l in range(layers):
        w_qkv, w_out, w_gu, w_down = weights[l]
        normed = move.gather((x * rms(x) * gain_a[l]).astype(BF))
        q, kv, proj = qkv_call(normed, w_qkv, gain_q[l], gain_k[l], cs, sn, nq, nk)
        kv_sib = move.sibling(kv)
        attended = attend_call(place, q, kv, kv_sib, segk, segq, reps, nk)
        middle = x + move.scatter(lambda d: dot(attended[d * t : (d + 1) * t], w_out))
        normed_mid = jnp.concatenate(move.gather((middle * rms(middle) * gain_m[l]).astype(BF)), axis=0)
        gate_up = dot(normed_mid, w_gu)
        hidden = (jax.nn.silu(gate_up[:, :ffr]) * gate_up[:, ffr:]).astype(BF)
        saved.append((x, normed, q, kv, kv_sib, proj, attended, middle, normed_mid, gate_up, hidden))
        x = middle + move.scatter(lambda d: dot(hidden[d * t : (d + 1) * t], w_down))
    outputs = move.turn(x.astype(BF))

    g = top.astype(F32)
    branch = top
    grads = [None] * layers
    for l in reversed(range(layers)):
        w_qkv, w_out, w_gu, w_down = weights[l]
        x, normed, q, kv, kv_sib, proj, attended, middle, normed_mid, gate_up, hidden = saved[l]
        branch = jnp.concatenate(move.gather(branch), axis=0)
        d_hidden = dot_cols(branch, w_down)
        gate, up = gate_up[:, :ffr], gate_up[:, ffr:]
        sig = jax.nn.sigmoid(gate)
        d_gate_up = jnp.concatenate(
            [
                (d_hidden * up * sig * (1.0 + gate * (1.0 - sig))).astype(BF),
                (d_hidden * (gate * sig)).astype(BF),
            ],
            axis=1,
        )
        d_normed_mid = move.scatter(lambda d: dot_cols(d_gate_up[d * t : (d + 1) * t], w_gu))
        d_middle = g + rms_back(middle, gain_m[l], d_normed_mid)
        out_branch = jnp.concatenate(move.gather(d_middle.astype(BF)), axis=0)
        down_g = dot_rows(hidden, branch).astype(BF)
        gu_g = dot_rows(normed_mid, d_gate_up).astype(BF)
        gu_g = lax.psum_scatter(gu_g, "ctx", scatter_dimension=0, tiled=True)
        d_attended = dot_cols(out_branch, w_out).astype(BF)
        dq, dko, dvo, dks, dvs = attend_back_call(place, q, kv, kv_sib, d_attended, segk, segq, reps, nk)
        dkv_sib = move.sibling(jnp.concatenate([dks, dvs], axis=1))
        out_g = dot_rows(attended, out_branch).astype(BF)
        row_g = jnp.concatenate([by_place(out_g), by_place(down_g)], axis=1)
        row_g = lax.psum_scatter(row_g, "ctx", scatter_dimension=0, tiled=False)
        d_proj, dqg, dkg = head_back_call(
            dq, dko, dvo, dkv_sib[:, : nk * HEAD], dkv_sib[:, nk * HEAD :], proj, cs, sn, gain_q[l], gain_k[l],
            reps, nq, nk,
        )
        d_normed = move.scatter(lambda d: dot_cols(d_proj[d * t : (d + 1) * t], w_qkv))
        qkv_g = dot_rows(jnp.concatenate(normed, axis=0), d_proj).astype(BF)
        qkv_g = lax.psum_scatter(qkv_g, "ctx", scatter_dimension=0, tiled=True)
        g = d_middle + rms_back(x, gain_a[l], d_normed)
        branch = g.astype(BF)
        grads[l] = (qkv_g, gu_g, row_g, dqg, dkg)
    input_grad = move.turn(branch).astype(F32)

    head_gains = jnp.concatenate([jnp.concatenate(grads[l][3:], axis=0) for l in range(layers)], axis=0)
    head_gains = lax.psum(head_gains, AXES).reshape(layers, 2, ctxs, HEAD // ctxs)
    head_gains = lax.dynamic_index_in_dim(head_gains, lax.axis_index("ctx"), axis=2, keepdims=False)

    full = []
    for l in range(layers):
        qkv_g, gu_g, row_g, _, _ = grads[l]
        row_g = move.turn(row_g)
        parts = [move.gather(v) for v in (qkv_g, gu_g, row_g)]

        def ordered(pieces, cut):
            stack = jnp.stack([cut(p) for p in pieces])
            return [lax.dynamic_index_in_dim(stack, k ^ r, axis=0, keepdims=False) for k in range(reps)]

        def across(pieces, cuts):
            return jnp.concatenate(
                [p for lo, hi in cuts for p in ordered(pieces, lambda v: v[:, lo:hi])], axis=1
            ).astype(F32)

        a, b = nq * HEAD, (nq + nk) * HEAD
        qkv_full = across(parts[0], ((0, a), (a, b), (b, b + nk * HEAD)))
        gu_full = across(parts[1], ((0, ffr), (ffr, 2 * ffr)))
        out_full = jnp.concatenate(ordered(parts[2], lambda v: v[:out_rows]), axis=0).astype(F32)
        down_full = jnp.concatenate(ordered(parts[2], lambda v: v[out_rows:]), axis=0).astype(F32)
        attn_g = jnp.sum(qkv_weight[l].astype(F32) * qkv_full, axis=1) / attn_gain[l].astype(F32)
        mlp_g = jnp.sum(gate_up_weight[l].astype(F32) * gu_full, axis=1) / mlp_gain[l].astype(F32)
        full.append((qkv_full, out_full, attn_g, head_gains[l, 0], head_gains[l, 1], mlp_g, gu_full, down_full))
    stacked_grads = [jnp.stack([full[l][i] for l in range(layers)]) for i in range(8)]
    return (outputs[None], input_grad[None], *stacked_grads)


def solution(mesh):
    return jax.shard_map(
        partial(local, mesh.shape["rep"], mesh.shape["ctx"]),
        mesh=mesh,
        in_specs=(
            P("rep", "ctx", None),
            P("rep", None),
            P("rep", None),
            P("rep", "ctx", None),
            P(None, "ctx", None),
            P(None, "ctx", None),
            P(None, "ctx"),
            P(None, "ctx"),
            P(None, "ctx"),
            P(None, "ctx"),
            P(None, "ctx", None),
            P(None, "ctx", None),
        ),
        out_specs=(
            P("rep", "ctx", None),
            P("rep", "ctx", None),
            P(None, "ctx", None),
            P(None, "ctx", None),
            P(None, "ctx"),
            P(None, "ctx"),
            P(None, "ctx"),
            P(None, "ctx"),
            P(None, "ctx", None),
            P(None, "ctx", None),
        ),
        check_vma=False,
    )
```
